32 devices in a mesh: groups: 2 (over y), inst: 4 (over z), section: 2 (over x), tp: 2 (over core).
Axes of the slice: x: 2, y: 2, z: 4, core: 2. Of those that a mesh axis runs over, the one named last changes fastest.
Arguments:
- emb: bfloat16 [4, 32, 8192], P(None, ('groups', 'inst'), 'tp'), parts along dimension 1, may hold values from -24 to 24
- attn_gain: float32 [2, 8192], P('section', 'tp'), may hold values from 0.1 to 1.9
- out_gain: float32 [2, 8192], P('section', 'tp'), may hold values from 0.4 to 1.6
- k_cache: bfloat16 [8, 2, 24, 128, 1024], P(('groups', 'inst'), 'section', None, None, 'tp'), parts along dimension 0, may hold values from -128 to 128
- v_cache: bfloat16 [8, 2, 24, 128, 1024], P(('groups', 'inst'), 'section', None, None, 'tp'), parts along dimension 0, may hold values from -6 to 6
- tables: int32 [8, 4, 6], P(('groups', 'inst')), parts along dimension 0, may hold values from 0 to 23, as said below
- lens: int32 [8, 4], P('groups'), parts along dimension 0, may hold values from 2 to 764
- partner: int32 [4], replicated, may hold values from 0 to 3, as said below
- mig_req: int32 [8], P('groups'), parts along dimension 0, may hold values from 0 to 3
Outputs:
- layer_out: bfloat16 [2, 4, 32, 8192], P('section', None, ('groups', 'inst'), 'tp'), parts along dimension 2
- arrived_k: bfloat16 [8, 2, 768, 1024], P(('groups', 'inst'), 'section', None, 'tp'), parts along dimension 0
- arrived_v: bfloat16 [8, 2, 768, 1024], P(('groups', 'inst'), 'section', None, 'tp'), parts along dimension 0
The draws below stay inside these ranges and needn't reach their ends.
There are 2 independent parts, one for each index of `groups`. The reference program is written for one: setup_inputs(seed, part) draws one part's arguments, and reference() takes and returns one part's arrays. A program takes and returns all parts, laid end to end along the dimension named above; an argument that names none is the same for every part. Nothing has to cross between parts.
Inputs may be any that keep to these rules, and one draw needn't show every extreme that they name: partner[i] = i XOR m for one m of 1 .. 3, the same for every i. `tables`: each instance's table names each of its 24 pool blocks exactly once.
All inputs are finite; a program needn't handle non-finite values.
Results may differ from the reference program's by a relative error of at most 0.0061.
Values may be sent and summed in bfloat16 or wider, within the bound.
A program may use at most 64 MiB of HBM per device.

```python
import jax
import jax.numpy as jnp
from jax import lax

QH = 64
KVH = 8
HD = 128
BLK = 128
REQ = 4
MAXBLK = 6
STEPS = 4
D = 8192
KVD = 1024
LAYERS = 2
CTX = 768
NPOOL = 24
L_MAX = 764
N_INST = 4


def pool_tables(key):
    subkeys = jax.random.split(jax.random.fold_in(key, 11), N_INST)
    perms = jax.vmap(lambda subkey: jax.random.permutation(subkey, NPOOL))(subkeys)
    return perms.reshape(N_INST, REQ, MAXBLK).astype(jnp.int32)


def draw_emb(key, part):
    feats = jnp.arange(D)
    rough = jnp.exp(jax.random.uniform(jax.random.fold_in(key, 21), (D,), jnp.float32, -0.35, 0.35))
    scales = jnp.where(feats < D // 2, 0.6, 1.2) * rough
    noise = jax.random.normal(jax.random.fold_in(key, 22), (STEPS, N_INST * REQ, D), jnp.float32)
    values = noise * scales
    return jnp.clip(values, -24.0, 24.0).astype(jnp.bfloat16)


def draw_out_gain(key, part):
    feats = jnp.arange(D)
    unit = jax.random.uniform(jax.random.fold_in(key, 31), (LAYERS, D), jnp.float32)
    low = jnp.where(feats < D // 2, 0.4, 0.8)
    return (low * jnp.exp(unit * jnp.log(2.0))).astype(jnp.float32)


def draw_k_cache(key, part):
    base = jax.random.normal(jax.random.fold_in(key, 41), (N_INST, LAYERS, NPOOL, BLK, KVD), jnp.float32)
    base = jnp.clip(base, -6.0, 6.0)
    return base.astype(jnp.bfloat16)


def draw_tables(key, part):
    return pool_tables(key)


def draw_lens(key, part):
    values = jax.random.randint(jax.random.fold_in(key, 13), (N_INST * REQ,), 2, L_MAX + 1, jnp.int32)
    longest = jax.random.randint(jax.random.fold_in(key, 14), (), 0, N_INST * REQ, jnp.int32)
    values = values.at[longest].set(L_MAX)
    return values.reshape(N_INST, REQ)


def draw_partner(key, part):
    offset = jax.random.randint(jax.random.fold_in(key, 15), (), 1, N_INST, jnp.int32)
    return jnp.bitwise_xor(jnp.arange(N_INST, dtype=jnp.int32), offset)


def set_ends(array, own_key, low, high):
    spot = [jax.random.randint(jax.random.fold_in(own_key, axis), (), 0, length) for axis, length in enumerate(array.shape)]
    widest = array.shape.index(max(array.shape))
    neighbour = spot[:widest] + [(spot[widest] + 1) % array.shape[widest]] + spot[widest + 1:]
    return array.at[tuple(spot)].set(low).at[tuple(neighbour)].set(high)


def steps_of(key, shape, cuts, smallest, largest):
    level, own = 1.0, jax.random.fold_in(key, 6)
    for position, blocks in cuts:
        heights = jnp.exp(jax.random.uniform(jax.random.fold_in(own, position), (blocks,), jnp.float32, smallest / len(cuts), largest / len(cuts)))
        level = level * jnp.repeat(heights, shape[position] // blocks).reshape([-1 if axis == position else 1 for axis in range(len(shape))])
    return level


def gaussian(own_key, dims, scale, limit, cuts=(), kind=jnp.bfloat16):
    values = jax.random.normal(own_key, dims, jnp.float32) * scale
    if len(cuts) > 0:
        values = steps_of(own_key, dims, cuts, -0.22, 0.18) * values
    return jnp.clip(values, min=-limit, max=limit).astype(kind)


def setup_inputs(seed: int = 0, part: int = 0) -> dict:
    key_list = jax.random.split(jax.random.key(seed), 10)
    own_keys = jax.random.split(jax.random.fold_in(key_list[9], part), 10)
    emb = draw_emb(jax.random.fold_in(jax.random.fold_in(key_list[9], part), 71), part)
    attn_gain = jnp.clip(1.0 + 0.18 * jax.random.normal(key_list[1], (LAYERS, D), jnp.float32), 0.1, 1.9)
    out_gain = draw_out_gain(jax.random.fold_in(key_list[9], 71), part)
    k_cache = draw_k_cache(jax.random.fold_in(jax.random.fold_in(key_list[9], part), 71), part)
    v_cache = gaussian(own_keys[4], (N_INST, LAYERS, NPOOL, BLK, KVD), 1.0, 6.0, ((0, 4), (1, 2), (4, 2)))
    tables = draw_tables(jax.random.fold_in(jax.random.fold_in(key_list[9], part), 71), part)
    lens = draw_lens(jax.random.fold_in(jax.random.fold_in(key_list[9], part), 71), part)
    partner = draw_partner(jax.random.fold_in(key_list[9], 71), part)
    mig_req = set_ends(jax.random.randint(own_keys[8], (N_INST,), 0, REQ), jax.random.fold_in(own_keys[8], 1), 0, REQ - 1).astype(jnp.int32)
    return dict(emb=emb, attn_gain=attn_gain, out_gain=out_gain, k_cache=k_cache, v_cache=v_cache, tables=tables, lens=lens, partner=partner, mig_req=mig_req)


def layer_keys(cache_layer, tables):

    def one_instance(pool_blocks, table_rows):
        return pool_blocks[table_rows.reshape(-1)].reshape(REQ, CTX, KVD)
    return jax.vmap(one_instance)(cache_layer, tables)

def reference(emb, attn_gain, out_gain, k_cache, v_cache, tables, lens, partner, mig_req):
    rows = N_INST * REQ
    group = QH // KVH
    scale = HD ** (-0.5)
    lens_flat = lens.reshape(rows)
    positions = jnp.arange(CTX, dtype=jnp.int32)
    old_mask = positions[None, :] < lens_flat[:, None]
    step_index = jnp.arange(STEPS, dtype=jnp.int32)
    new_keys = jnp.zeros((LAYERS, STEPS, rows, KVD), jnp.bfloat16)
    new_values = jnp.zeros((LAYERS, STEPS, rows, KVD), jnp.bfloat16)
    results = [[None] * STEPS for layer in range(LAYERS)]
    for step in range(STEPS):
        hidden = emb[step]
        for layer in range(LAYERS):
            hidden_f = hidden.astype(jnp.float32)
            squares = lax.optimization_barrier(jnp.sum(hidden_f * hidden_f, axis=-1))
            normed = hidden_f * lax.rsqrt(squares / D + 1e-05)[:, None] * attn_gain[layer]
            heads = normed.reshape(rows, KVH, group, HD)
            query = heads.astype(jnp.bfloat16)
            key_step = lax.optimization_barrier(jnp.mean(heads, axis=2)).reshape(rows, KVD).astype(jnp.bfloat16)
            value_step = lax.optimization_barrier(jnp.mean(hidden_f.reshape(rows, KVH, group, HD), axis=2)).reshape(rows, KVD).astype(jnp.bfloat16)
            new_keys = new_keys.at[layer, step].set(key_step)
            new_values = new_values.at[layer, step].set(value_step)
            keys_old = layer_keys(k_cache[:, layer], tables).reshape(rows, CTX, KVH, HD)
            values_old = layer_keys(v_cache[:, layer], tables).reshape(rows, CTX, KVH, HD)
            keys_fresh = new_keys[layer].reshape(STEPS, rows, KVH, HD)
            values_fresh = new_values[layer].reshape(STEPS, rows, KVH, HD)
            query_f = query.astype(jnp.float32)
            score_old = jnp.einsum('rgqd,rcgd->rgqc', query_f, keys_old.astype(jnp.float32)) * scale
            score_old = jnp.where(old_mask[:, None, None, :], score_old, -jnp.inf)
            score_new = jnp.einsum('rgqd,trgd->rgqt', query_f, keys_fresh.astype(jnp.float32)) * scale
            score_new = jnp.where((step_index <= step)[None, None, None, :], score_new, -jnp.inf)
            top = jnp.maximum(lax.optimization_barrier(jnp.max(score_old, axis=-1)), lax.optimization_barrier(jnp.max(score_new, axis=-1)))
            expo_old = jnp.exp(score_old - top[..., None])
            expo_new = jnp.exp(score_new - top[..., None])
            total = lax.optimization_barrier(jnp.sum(expo_old, axis=-1)) + lax.optimization_barrier(jnp.sum(expo_new, axis=-1))
            weight_old = (expo_old / total[..., None]).astype(jnp.bfloat16)
            weight_new = (expo_new / total[..., None]).astype(jnp.bfloat16)
            attended = jnp.einsum('rgqc,rcgd->rgqd', weight_old.astype(jnp.float32), values_old.astype(jnp.float32))
            attended = attended + jnp.einsum('rgqt,trgd->rgqd', weight_new.astype(jnp.float32), values_fresh.astype(jnp.float32))
            head_norm = attended * lax.rsqrt(lax.optimization_barrier(jnp.mean(attended * attended, axis=-1)) + 1e-05)[..., None]
            hidden = (hidden_f + head_norm.reshape(rows, D) * out_gain[layer]).astype(jnp.bfloat16)
            results[layer][step] = hidden
    layer_out = jnp.stack([jnp.stack(results[layer]) for layer in range(LAYERS)])
    source = partner
    chosen = mig_req[source]
    length = lens[source, chosen]
    flat_index = source * REQ + chosen

    def place(base, piece, start):
        return lax.dynamic_update_slice(base, piece, (start, jnp.int32(0)))
    arrived = []
    for cache, fresh_all in ((k_cache, new_keys), (v_cache, new_values)):
        per_layer = []
        for layer in range(LAYERS):
            logical = layer_keys(cache[:, layer], tables)
            picked = logical[source, chosen]
            picked = jnp.where(positions[None, :, None] < length[:, None, None], picked, jnp.zeros((), picked.dtype))
            fresh = jnp.transpose(fresh_all[layer][:, flat_index], (1, 0, 2))
            per_layer.append(jax.vmap(place)(picked, fresh, length))
        arrived.append(jnp.stack(per_layer, axis=1))
    return (layer_out, arrived[0], arrived[1])
```

```python
import functools

import jax
import jax.numpy as jnp
from jax import lax
from jax.experimental import pallas as pl
from jax.experimental.pallas import tpu as pltpu
from jax.sharding import PartitionSpec as P

QH = 64
KVH = 8
HD = 128
LOADS = 6
PAD = 8
MESH = pl.DeviceIdType.MESH


def fused(offset, tables, lens, mig_req, emb, gain_attn, gain_out, k_hbm, v_hbm,
          res, out_k, out_v,
          k_all, v_all, send_buf, recv_buf, fresh_send, fresh_recv,
          h32, h_in, ss_all, ss_out, fk, fv, q_buf, o_buf,
          load_sem, mig_send, mig_recv, fresh_ssem, fresh_rsem,
          h_ssem, h_rsem, ss_ssem, ss_rsem, peer_sem):
    sections = lax.axis_size("section")
    cores = lax.axis_size("tp")
    section = lax.axis_index("section")
    core = lax.axis_index("tp")
    inst = lax.axis_index("inst")
    steps, requests, width = emb.shape
    pool, blk, kv_local = k_all.shape
    maxblk = tables.shape[2]
    heads_kv = kv_local // HD
    group = QH // KVH
    rows = group * steps
    scale = HD ** (-0.5)
    total_width = width * cores
    source = jnp.bitwise_xor(inst, offset)

    part = pool // LOADS
    loads = []
    for which, (src, dst) in enumerate(((k_hbm, k_all), (v_hbm, v_all))):
        for i in range(LOADS):
            span = pl.ds(i * part, part)
            loads.append(pltpu.make_async_copy(src.at[0, 0, span], dst.at[span], load_sem.at[which, i]))
    for copy in loads:
        copy.start()

    barrier = pltpu.get_barrier_semaphore()
    pl.semaphore_signal(barrier, inc=1, device_id={"inst": source}, device_id_type=MESH)
    for step in range(1, cores):
        pl.semaphore_signal(barrier, inc=1, device_id={"tp": lax.rem(core + step, cores)}, device_id_type=MESH)

    @pl.when(section > 0)
    def _():
        for other in range(cores):
            pl.semaphore_signal(barrier, inc=1, device_id={"section": section - 1, "tp": other}, device_id_type=MESH)

    @pl.when(section < sections - 1)
    def _():
        for other in range(cores):
            pl.semaphore_signal(barrier, inc=1, device_id={"section": section + 1, "tp": other}, device_id_type=MESH)

    neighbours = jnp.minimum(section, 1) + jnp.minimum(sections - 1 - section, 1)
    pl.semaphore_wait(barrier, cores * (1 + neighbours))

    def peer_copy(r, step):
        return pltpu.make_async_remote_copy(
            src_ref=ss_all.at[core, r], dst_ref=ss_all.at[core, r],
            send_sem=peer_sem.at[r, step], recv_sem=ss_rsem.at[r, core],
            device_id={"tp": lax.rem(core + step, cores)}, device_id_type=MESH)

    def next_copy(r):
        return pltpu.make_async_remote_copy(
            src_ref=res.at[r], dst_ref=h_in.at[r],
            send_sem=h_ssem.at[r], recv_sem=h_rsem.at[r],
            device_id={"section": section + 1}, device_id_type=MESH)

    def next_sum(r, other):
        return pltpu.make_async_remote_copy(
            src_ref=ss_out.at[r], dst_ref=ss_all.at[core, r],
            send_sem=ss_ssem.at[r, other], recv_sem=ss_rsem.at[r, core],
            device_id={"section": section + 1, "tp": other}, device_id_type=MESH)

    def sum_arrival(r, other):
        return pltpu.make_async_remote_copy(
            src_ref=ss_out.at[r], dst_ref=ss_all.at[other, r],
            send_sem=ss_ssem.at[r, other], recv_sem=ss_rsem.at[r, other],
            device_id={"tp": lax.rem(core + 1, cores)}, device_id_type=MESH)

    def mig_copy(which, b):
        return pltpu.make_async_remote_copy(
            src_ref=send_buf.at[which, b], dst_ref=recv_buf.at[which, b],
            send_sem=mig_send.at[which, b], recv_sem=mig_recv.at[which, b],
            device_id={"inst": source}, device_id_type=MESH)

    fresh_copy = pltpu.make_async_remote_copy(
        src_ref=fresh_send, dst_ref=fresh_recv, send_sem=fresh_ssem, recv_sem=fresh_rsem,
        device_id={"inst": source}, device_id_type=MESH)

    @pl.when(section == 0)
    def _():
        for t in range(steps):
            e = emb[t].astype(jnp.float32)
            for r in range(requests):
                h32[r, t:t + 1, :] = e[r:r + 1, :]
        for r in range(requests):
            h = h32[r]
            ss_all[core, r] = jnp.broadcast_to(jnp.sum(h * h, axis=-1, keepdims=True), (steps, HD))
        for r in range(requests):
            for step in range(1, cores):
                peer_copy(r, step).start()

    fk[...] = jnp.zeros_like(fk)
    fv[...] = jnp.zeros_like(fv)
    handed = mig_req[inst]
    for which, stored in enumerate((k_all, v_all)):
        for i in range(LOADS):
            loads[which * LOADS + i].wait()

        def send_block(b, carry, which=which, stored=stored):
            send_buf[which, b] = stored[tables[0, handed, b]]
            mig_copy(which, b).start()
            return carry
        lax.fori_loop(0, maxblk, send_block, 0)

    def one_request(r, carry):
        @pl.when(section == 0)
        def _():
            for step in range(1, cores):
                sum_arrival(r, lax.rem(core + step, cores)).wait_recv()

        @pl.when(section > 0)
        def _():
            next_copy(r).wait_recv()
            for other in range(cores):
                sum_arrival(r, other).wait_recv()
            h32[r] = h_in[r].astype(jnp.float32)

        squares = ss_all[0, r]
        for other in range(1, cores):
            squares = squares + ss_all[other, r]
        ratio = lax.rsqrt(squares / total_width + 1e-05)
        length = lens[inst, r]
        for g in range(heads_kv):
            key_sum = jnp.zeros((steps, HD), jnp.float32)
            value_sum = jnp.zeros((steps, HD), jnp.float32)
            for j in range(group):
                lanes = slice((g * group + j) * HD, (g * group + j + 1) * HD)
                hj = h32[r, :, lanes]
                xj = hj * ratio * gain_attn[0:1, lanes]
                q_buf[g, j * steps:(j + 1) * steps, :] = xj
                key_sum = key_sum + xj
                value_sum = value_sum + hj
            fk[r, 0:steps, g * HD:(g + 1) * HD] = key_sum * (1.0 / group)
            fv[r, 0:steps, g * HD:(g + 1) * HD] = value_sum * (1.0 / group)
        col = lax.broadcasted_iota(jnp.int32, (rows, blk), 1)
        new_col = lax.broadcasted_iota(jnp.int32, (rows, PAD), 1)
        new_step = lax.rem(lax.broadcasted_iota(jnp.int32, (rows, PAD), 0), steps)
        for g in range(heads_kv):
            lanes = slice(g * HD, (g + 1) * HD)
            q = q_buf[g].astype(jnp.bfloat16)
            nt = (((1,), (1,)), ((), ()))
            scores = []
            for b in range(maxblk):
                kb = k_all[tables[0, r, b], :, lanes]
                s = lax.dot_general(q, kb, nt, preferred_element_type=jnp.float32) * scale
                scores.append(jnp.where(col + b * blk < length, s, -jnp.inf))
            new = lax.dot_general(q, fk[r, :, lanes].astype(jnp.bfloat16), nt, preferred_element_type=jnp.float32) * scale
            new = jnp.where(new_col <= new_step, new, -jnp.inf)
            top = functools.reduce(jnp.maximum, scores)
            top = jnp.maximum(jnp.max(top, axis=-1, keepdims=True), jnp.max(new, axis=-1, keepdims=True))
            expo = [jnp.exp(s - top) for s in scores]
            expo_new = jnp.exp(new - top)
            total = jnp.sum(functools.reduce(jnp.add, expo), axis=-1, keepdims=True)
            total = total + jnp.sum(expo_new, axis=-1, keepdims=True)
            inverse = 1.0 / total
            o = jnp.dot((expo_new * inverse).astype(jnp.bfloat16), fv[r, :, lanes].astype(jnp.bfloat16),
                        preferred_element_type=jnp.float32)
            for b in range(maxblk):
                vb = v_all[tables[0, r, b], :, lanes]
                o = o + jnp.dot((expo[b] * inverse).astype(jnp.bfloat16), vb, preferred_element_type=jnp.float32)
            o_buf[g] = o * lax.rsqrt(jnp.mean(o * o, axis=-1, keepdims=True) + 1e-05)
        sums = jnp.zeros((steps, HD), jnp.float32)
        for g in range(heads_kv):
            for j in range(group):
                lanes = slice((g * group + j) * HD, (g * group + j + 1) * HD)
                y = h32[r, :, lanes] + o_buf[g, j * steps:(j + 1) * steps, :] * gain_out[0:1, lanes]
                y = y.astype(jnp.bfloat16)
                res[r, :, lanes] = y
                y = y.astype(jnp.float32)
                sums = sums + y * y
        ss_out[r] = jnp.broadcast_to(jnp.sum(sums, axis=-1, keepdims=True), (steps, HD))

        @pl.when(section < sections - 1)
        def _():
            next_copy(r).start()
            for other in range(cores):
                next_sum(r, other).start()
        return carry

    lax.fori_loop(0, requests, one_request, 0)

    fresh_send[0] = fk[handed].astype(jnp.bfloat16)
    fresh_send[1] = fv[handed].astype(jnp.bfloat16)
    fresh_copy.start()
    fresh_copy.wait_recv()
    source_len = lens[source, mig_req[source]]

    for which in range(2):
        def settle(b, carry, which=which):
            mig_copy(which, b).wait_recv()
            pos = lax.broadcasted_iota(jnp.int32, (blk, PAD), 0) + b * blk - source_len
            hit = jnp.where(pos == lax.broadcasted_iota(jnp.int32, (blk, PAD), 1), 1.0, 0.0).astype(jnp.bfloat16)
            placed = jnp.dot(hit, fresh_recv[which], preferred_element_type=jnp.float32)
            row = lax.broadcasted_iota(jnp.int32, (blk, kv_local), 0) + b * blk
            block = jnp.where(row < source_len, recv_buf[which, b].astype(jnp.float32), placed)
            target = (out_k, out_v)[which]
            target[0, 0, pl.ds(pl.multiple_of(b * blk, blk), blk), :] = block.astype(jnp.bfloat16)
            return carry
        lax.fori_loop(0, maxblk, settle, 0)

    for which in range(2):
        def finish(b, carry, which=which):
            mig_copy(which, b).wait_send()
            return carry
        lax.fori_loop(0, maxblk, finish, 0)
    fresh_copy.wait_send()

    @pl.when(section == 0)
    def _():
        for r in range(requests):
            for step in range(1, cores):
                peer_copy(r, step).wait_send()

    @pl.when(section < sections - 1)
    def _():
        for r in range(requests):
            next_copy(r).wait_send()
            for other in range(cores):
                next_sum(r, other).wait_send()


def local(emb, attn_gain, out_gain, k_cache, v_cache, tables, lens, partner, mig_req):
    steps, requests, width = emb.shape
    _, _, pool, blk, kv_local = k_cache.shape
    maxblk = tables.shape[2]
    cores = lax.axis_size("tp")
    context = maxblk * blk
    rows = QH // KVH * steps
    heads_kv = kv_local // HD
    bf16, f32 = jnp.bfloat16, jnp.float32
    smem = pl.BlockSpec(memory_space=pltpu.SMEM)
    vmem = pl.BlockSpec(memory_space=pltpu.VMEM)
    anywhere = pl.BlockSpec(memory_space=pl.ANY)
    dma = pltpu.SemaphoreType.DMA

    def call(offset):
        return pl.pallas_call(
            functools.partial(fused, offset),
            out_shape=(
                jax.ShapeDtypeStruct((requests, steps, width), bf16),
                jax.ShapeDtypeStruct((1, 1, context, kv_local), bf16),
                jax.ShapeDtypeStruct((1, 1, context, kv_local), bf16),
            ),
            in_specs=[smem, smem, smem, vmem, vmem, vmem, anywhere, anywhere],
            out_specs=(vmem, vmem, vmem),
            scratch_shapes=[
                pltpu.VMEM((pool, blk, kv_local), bf16),
                pltpu.VMEM((pool, blk, kv_local), bf16),
                pltpu.VMEM((2, maxblk, blk, kv_local), bf16),
                pltpu.VMEM((2, maxblk, blk, kv_local), bf16),
                pltpu.VMEM((2, PAD, kv_local), bf16),
                pltpu.VMEM((2, PAD, kv_local), bf16),
                pltpu.VMEM((requests, steps, width), f32),
                pltpu.VMEM((requests, steps, width), bf16),
                pltpu.VMEM((cores, requests, steps, HD), f32),
                pltpu.VMEM((requests, steps, HD), f32),
                pltpu.VMEM((requests, PAD, kv_local), f32),
                pltpu.VMEM((requests, PAD, kv_local), f32),
                pltpu.VMEM((heads_kv, rows, HD), f32),
                pltpu.VMEM((heads_kv, rows, HD), f32),
                dma((2, LOADS)),
                dma((2, maxblk)),
                dma((2, maxblk)),
                dma,
                dma,
                dma((requests,)),
                dma((requests,)),
                dma((requests, cores)),
                dma((requests, cores)),
                dma((requests, cores)),
            ],
            compiler_params=pltpu.CompilerParams(collective_id=offset, has_side_effects=True),
        )

    offsets = lax.axis_size("inst") - 1
    branches = [call(offset) for offset in range(1, offsets + 1)]
    chosen = jnp.clip(partner[0] - 1, 0, offsets - 1)
    res, arrived_k, arrived_v = lax.switch(
        chosen, branches, tables, lens, mig_req, emb, attn_gain, out_gain, k_cache, v_cache)
    return jnp.swapaxes(res, 0, 1)[None], arrived_k, arrived_v


def solution(mesh):
    return jax.shard_map(
        local,
        mesh=mesh,
        in_specs=(
            P(None, ("groups", "inst"), "tp"),
            P("section", "tp"),
            P("section", "tp"),
            P(("groups", "inst"), "section", None, None, "tp"),
            P(("groups", "inst"), "section", None, None, "tp"),
            P(("groups", "inst"), None, None),
            P("groups", None),
            P(),
            P("groups"),
        ),
        out_specs=(
            P("section", None, ("groups", "inst"), "tp"),
            P(("groups", "inst"), "section", None, "tp"),
            P(("groups", "inst"), "section", None, "tp"),
        ),
        check_vma=False,
    )
```

```python
import functools

import jax
import jax.numpy as jnp
from jax import lax
from jax.experimental import pallas as pl
from jax.experimental.pallas import tpu as pltpu
from jax.sharding import PartitionSpec as P

QH = 64
KVH = 8
HD = 128
LOADS = 6
STORES = 2
PAD = 8
MESH = pl.DeviceIdType.MESH


def fused(offset, tables_hbm, lens_hbm, mig_hbm, emb_hbm, gain_attn_hbm, gain_out_hbm, k_hbm, v_hbm,
          out, out_k, out_v,
          tables, lens, mig_req, emb, gain_attn, gain_out, res, turn,
          k_all, v_all, send_buf, recv_buf, fresh_send, fresh_recv,
          h32, h_in, ss_all, ss_out, fk, fv, q_buf, o_buf,
          small_sem, load_sem, mig_send, mig_recv, fresh_ssem, fresh_rsem,
          h_ssem, h_rsem, ss_ssem, ss_rsem, peer_sem):
    sections = lax.axis_size("section")
    cores = lax.axis_size("tp")
    section = lax.axis_index("section")
    core = lax.axis_index("tp")
    inst = lax.axis_index("inst")
    steps, requests, width = emb.shape
    pool, blk, kv_local = k_all.shape
    maxblk = tables.shape[2]
    heads_kv = kv_local // HD
    group = QH // KVH
    rows = group * steps
    scale = HD ** (-0.5)
    total_width = width * cores
    source = jnp.bitwise_xor(inst, offset)

    part = pool // LOADS
    loads = []
    for which, (src, dst) in enumerate(((k_hbm, k_all), (v_hbm, v_all))):
        for i in range(LOADS):
            span = pl.ds(i * part, part)
            loads.append(pltpu.make_async_copy(src.at[0, 0, span], dst.at[span], load_sem.at[which, i]))
    small = []
    for i, (src, dst) in enumerate((
            (tables_hbm, tables), (mig_hbm, mig_req), (lens_hbm, lens),
            (emb_hbm, emb), (gain_attn_hbm, gain_attn), (gain_out_hbm, gain_out))):
        small.append(pltpu.make_async_copy(src, dst, small_sem.at[i]))
    for copy in small[:2] + loads[:LOADS] + small[2:]:
        copy.start()

    barrier = pltpu.get_barrier_semaphore()
    pl.semaphore_signal(barrier, inc=1, device_id={"inst": source}, device_id_type=MESH)
    for step in range(1, cores):
        pl.semaphore_signal(barrier, inc=1, device_id={"tp": lax.rem(core + step, cores)}, device_id_type=MESH)

    @pl.when(section > 0)
    def _():
        for other in range(cores):
            pl.semaphore_signal(barrier, inc=1, device_id={"section": section - 1, "tp": other}, device_id_type=MESH)

    @pl.when(section < sections - 1)
    def _():
        for other in range(cores):
            pl.semaphore_signal(barrier, inc=1, device_id={"section": section + 1, "tp": other}, device_id_type=MESH)

    neighbours = jnp.minimum(section, 1) + jnp.minimum(sections - 1 - section, 1)
    pl.semaphore_wait(barrier, cores * (1 + neighbours))

    def peer_copy(r, step):
        return pltpu.make_async_remote_copy(
            src_ref=ss_all.at[core, r], dst_ref=ss_all.at[core, r],
            send_sem=peer_sem.at[r, step], recv_sem=ss_rsem.at[r, core],
            device_id={"tp": lax.rem(core + step, cores)}, device_id_type=MESH)

    def next_copy(r):
        return pltpu.make_async_remote_copy(
            src_ref=res.at[r], dst_ref=h_in.at[r],
            send_sem=h_ssem.at[r], recv_sem=h_rsem.at[r],
            device_id={"section": section + 1}, device_id_type=MESH)

    def next_sum(r, other):
        return pltpu.make_async_remote_copy(
            src_ref=ss_out.at[r], dst_ref=ss_all.at[core, r],
            send_sem=ss_ssem.at[r, other], recv_sem=ss_rsem.at[r, core],
            device_id={"section": section + 1, "tp": other}, device_id_type=MESH)

    def sum_arrival(r, other):
        return pltpu.make_async_remote_copy(
            src_ref=ss_out.at[r], dst_ref=ss_all.at[other, r],
            send_sem=ss_ssem.at[r, other], recv_sem=ss_rsem.at[r, other],
            device_id={"tp": lax.rem(core + 1, cores)}, device_id_type=MESH)

    def mig_copy(which, b):
        return pltpu.make_async_remote_copy(
            src_ref=send_buf.at[which, b], dst_ref=recv_buf.at[which, b],
            send_sem=mig_send.at[which, b], recv_sem=mig_recv.at[which, b],
            device_id={"inst": source}, device_id_type=MESH)

    fresh_copy = pltpu.make_async_remote_copy(
        src_ref=fresh_send, dst_ref=fresh_recv, send_sem=fresh_ssem, recv_sem=fresh_rsem,
        device_id={"inst": source}, device_id_type=MESH)

    for copy in small[:2]:
        copy.wait()
    handed = mig_req[inst]
    for which, stored in enumerate((k_all, v_all)):
        for i in range(LOADS):
            loads[which * LOADS + i].wait()
        if which == 0:
            for copy in loads[LOADS:]:
                copy.start()

        def send_block(b, carry, which=which, stored=stored):
            send_buf[which, b] = stored[tables[0, handed, b]]
            mig_copy(which, b).start()
            return carry
        lax.fori_loop(0, maxblk, send_block, 0)

    for copy in small[2:]:
        copy.wait()

    @pl.when(section == 0)
    def _():
        for t in range(steps):
            e = emb[t].astype(jnp.float32)
            for r in range(requests):
                h32[r, t:t + 1, :] = e[r:r + 1, :]
        for r in range(requests):
            h = h32[r]
            ss_all[core, r] = jnp.broadcast_to(jnp.sum(h * h, axis=-1, keepdims=True), (steps, HD))
        for r in range(requests):
            for step in range(1, cores):
                peer_copy(r, step).start()

    fk[...] = jnp.zeros_like(fk)
    fv[...] = jnp.zeros_like(fv)

    def one_request(r, carry):
        @pl.when(section == 0)
        def _():
            for step in range(1, cores):
                sum_arrival(r, lax.rem(core + step, cores)).wait_recv()

        @pl.when(section > 0)
        def _():
            next_copy(r).wait_recv()
            for other in range(cores):
                sum_arrival(r, other).wait_recv()
            h32[r] = h_in[r].astype(jnp.float32)

        squares = ss_all[0, r]
        for other in range(1, cores):
            squares = squares + ss_all[other, r]
        ratio = lax.rsqrt(squares / total_width + 1e-05)
        length = lens[inst, r]
        for g in range(heads_kv):
            key_sum = jnp.zeros((steps, HD), jnp.float32)
            value_sum = jnp.zeros((steps, HD), jnp.float32)
            for j in range(group):
                lanes = slice((g * group + j) * HD, (g * group + j + 1) * HD)
                hj = h32[r, :, lanes]
                xj = hj * ratio * gain_attn[0:1, lanes]
                q_buf[g, j * steps:(j + 1) * steps, :] = xj
                key_sum = key_sum + xj
                value_sum = value_sum + hj
            fk[r, 0:steps, g * HD:(g + 1) * HD] = key_sum * (1.0 / group)
            fv[r, 0:steps, g * HD:(g + 1) * HD] = value_sum * (1.0 / group)
        col = lax.broadcasted_iota(jnp.int32, (rows, blk), 1)
        new_col = lax.broadcasted_iota(jnp.int32, (rows, PAD), 1)
        new_step = lax.rem(lax.broadcasted_iota(jnp.int32, (rows, PAD), 0), steps)
        for g in range(heads_kv):
            lanes = slice(g * HD, (g + 1) * HD)
            q = q_buf[g].astype(jnp.bfloat16)
            nt = (((1,), (1,)), ((), ()))
            scores = []
            for b in range(maxblk):
                kb = k_all[tables[0, r, b], :, lanes]
                s = lax.dot_general(q, kb, nt, preferred_element_type=jnp.float32) * scale
                scores.append(jnp.where(col + b * blk < length, s, -jnp.inf))
            new = lax.dot_general(q, fk[r, :, lanes].astype(jnp.bfloat16), nt, preferred_element_type=jnp.float32) * scale
            new = jnp.where(new_col <= new_step, new, -jnp.inf)
            top = functools.reduce(jnp.maximum, scores)
            top = jnp.maximum(jnp.max(top, axis=-1, keepdims=True), jnp.max(new, axis=-1, keepdims=True))
            expo = [jnp.exp(s - top) for s in scores]
            expo_new = jnp.exp(new - top)
            total = jnp.sum(functools.reduce(jnp.add, expo), axis=-1, keepdims=True)
            total = total + jnp.sum(expo_new, axis=-1, keepdims=True)
            inverse = 1.0 / total
            o = jnp.dot((expo_new * inverse).astype(jnp.bfloat16), fv[r, :, lanes].astype(jnp.bfloat16),
                        preferred_element_type=jnp.float32)
            for b in range(maxblk):
                vb = v_all[tables[0, r, b], :, lanes]
                o = o + jnp.dot((expo[b] * inverse).astype(jnp.bfloat16), vb, preferred_element_type=jnp.float32)
            o_buf[g] = o * lax.rsqrt(jnp.mean(o * o, axis=-1, keepdims=True) + 1e-05)
        sums = jnp.zeros((steps, HD), jnp.float32)
        for g in range(heads_kv):
            for j in range(group):
                lanes = slice((g * group + j) * HD, (g * group + j + 1) * HD)
                y = h32[r, :, lanes] + o_buf[g, j * steps:(j + 1) * steps, :] * gain_out[0:1, lanes]
                y = y.astype(jnp.bfloat16)
                res[r, :, lanes] = y
                y = y.astype(jnp.float32)
                sums = sums + y * y
        ss_out[r] = jnp.broadcast_to(jnp.sum(sums, axis=-1, keepdims=True), (steps, HD))

        @pl.when(section < sections - 1)
        def _():
            next_copy(r).start()
            for other in range(cores):
                next_sum(r, other).start()
        return carry

    lax.fori_loop(0, requests, one_request, 0)

    fresh_send[0] = fk[handed].astype(jnp.bfloat16)
    fresh_send[1] = fv[handed].astype(jnp.bfloat16)
    fresh_copy.start()
    for r in range(requests):
        y = res[r].astype(jnp.float32)
        for t in range(steps):
            turn[t, r:r + 1, :] = y[t:t + 1, :]
    out[0] = turn[...].astype(jnp.bfloat16)
    fresh_copy.wait_recv()
    source_len = lens[source, mig_req[source]]

    for which in range(2):
        def settle(b, carry, which=which):
            mig_copy(which, b).wait_recv()
            pos = lax.broadcasted_iota(jnp.int32, (blk, PAD), 0) + b * blk - source_len
            hit = jnp.where(pos == lax.broadcasted_iota(jnp.int32, (blk, PAD), 1), 1.0, 0.0).astype(jnp.bfloat16)
            placed = jnp.dot(hit, fresh_recv[which], preferred_element_type=jnp.float32)
            row = lax.broadcasted_iota(jnp.int32, (blk, kv_local), 0) + b * blk
            block = jnp.where(row < source_len, recv_buf[which, b].astype(jnp.float32), placed)
            target = (out_k, out_v)[which]
            target[0, 0, pl.ds(pl.multiple_of(b * blk, blk), blk), :] = block.astype(jnp.bfloat16)
            return carry
        lax.fori_loop(0, maxblk, settle, 0)

    for which in range(2):
        def finish(b, carry, which=which):
            mig_copy(which, b).wait_send()
            return carry
        lax.fori_loop(0, maxblk, finish, 0)
    fresh_copy.wait_send()

    @pl.when(section == 0)
    def _():
        for r in range(requests):
            for step in range(1, cores):
                peer_copy(r, step).wait_send()

    @pl.when(section < sections - 1)
    def _():
        for r in range(requests):
            next_copy(r).wait_send()
            for other in range(cores):
                next_sum(r, other).wait_send()


def store(res, k, v, res_out, k_out, v_out, sems, res_sem):
    part = k.shape[2] // STORES
    copies = [pltpu.make_async_copy(res, res_out, res_sem)]
    for which, (src, dst) in enumerate(((k, k_out), (v, v_out))):
        for i in range(STORES):
            span = pl.ds(i * part, part)
            copies.append(pltpu.make_async_copy(src.at[0, 0, span], dst.at[0, 0, span], sems.at[which, i]))
    for copy in copies:
        copy.start()
    for copy in copies:
        copy.wait()


def local(emb, attn_gain, out_gain, k_cache, v_cache, tables, lens, partner, mig_req):
    steps, requests, width = emb.shape
    _, _, pool, blk, kv_local = k_cache.shape
    maxblk = tables.shape[2]
    cores = lax.axis_size("tp")
    context = maxblk * blk
    rows = QH // KVH * steps
    heads_kv = kv_local // HD
    bf16, f32 = jnp.bfloat16, jnp.float32
    vmem = pl.BlockSpec(memory_space=pltpu.VMEM)
    anywhere = pl.BlockSpec(memory_space=pl.ANY)
    dma = pltpu.SemaphoreType.DMA

    def call(offset):
        return pl.pallas_call(
            functools.partial(fused, offset),
            out_shape=(
                jax.ShapeDtypeStruct((1, steps, requests, width), bf16),
                jax.ShapeDtypeStruct((1, 1, context, kv_local), bf16),
                jax.ShapeDtypeStruct((1, 1, context, kv_local), bf16),
            ),
            in_specs=[anywhere] * 8,
            out_specs=(vmem, vmem, vmem),
            scratch_shapes=[
                pltpu.SMEM(tables.shape, jnp.int32),
                pltpu.SMEM(lens.shape, jnp.int32),
                pltpu.SMEM(mig_req.shape, jnp.int32),
                pltpu.VMEM(emb.shape, bf16),
                pltpu.VMEM(attn_gain.shape, f32),
                pltpu.VMEM(out_gain.shape, f32),
                pltpu.VMEM((requests, steps, width), bf16),
                pltpu.VMEM((steps, requests, width), f32),
                pltpu.VMEM((pool, blk, kv_local), bf16),
                pltpu.VMEM((pool, blk, kv_local), bf16),
                pltpu.VMEM((2, maxblk, blk, kv_local), bf16),
                pltpu.VMEM((2, maxblk, blk, kv_local), bf16),
                pltpu.VMEM((2, PAD, kv_local), bf16),
                pltpu.VMEM((2, PAD, kv_local), bf16),
                pltpu.VMEM((requests, steps, width), f32),
                pltpu.VMEM((requests, steps, width), bf16),
                pltpu.VMEM((cores, requests, steps, HD), f32),
                pltpu.VMEM((requests, steps, HD), f32),
                pltpu.VMEM((requests, PAD, kv_local), f32),
                pltpu.VMEM((requests, PAD, kv_local), f32),
                pltpu.VMEM((heads_kv, rows, HD), f32),
                pltpu.VMEM((heads_kv, rows, HD), f32),
                dma((6,)),
                dma((2, LOADS)),
                dma((2, maxblk)),
                dma((2, maxblk)),
                dma,
                dma,
                dma((requests,)),
                dma((requests,)),
                dma((requests, cores)),
                dma((requests, cores)),
                dma((requests, cores)),
            ],
            compiler_params=pltpu.CompilerParams(collective_id=offset, has_side_effects=True),
        )

    offsets = lax.axis_size("inst") - 1
    branches = [call(offset) for offset in range(1, offsets + 1)]
    chosen = jnp.clip(partner[0] - 1, 0, offsets - 1)
    results = lax.switch(
        chosen, branches, tables, lens, mig_req, emb, attn_gain, out_gain, k_cache, v_cache)
    return pl.pallas_call(
        store,
        out_shape=tuple(jax.ShapeDtypeStruct(a.shape, a.dtype) for a in results),
        in_specs=[anywhere] * 3,
        out_specs=(anywhere,) * 3,
        scratch_shapes=[dma((2, STORES)), dma],
    )(*results)


def solution(mesh):
    return jax.shard_map(
        local,
        mesh=mesh,
        in_specs=(
            P(None, ("groups", "inst"), "tp"),
            P("section", "tp"),
            P("section", "tp"),
            P(("groups", "inst"), "section", None, None, "tp"),
            P(("groups", "inst"), "section", None, None, "tp"),
            P(("groups", "inst"), None, None),
            P("groups", None),
            P(),
            P("groups"),
        ),
        out_specs=(
            P("section", None, ("groups", "inst"), "tp"),
            P(("groups", "inst"), "section", None, "tp"),
            P(("groups", "inst"), "section", None, "tp"),
        ),
        check_vma=False,
    )
```

```python
import functools

import jax
import jax.numpy as jnp
from jax import lax
from jax.experimental import pallas as pl
from jax.experimental.pallas import tpu as pltpu
from jax.sharding import PartitionSpec as P

QH = 64
KVH = 8
HD = 128
LOADS = 6
STORES = 2
PAD = 8
MESH = pl.DeviceIdType.MESH


def fused(offset, tables_hbm, lens_hbm, mig_hbm, emb_hbm, gain_attn_hbm, gain_out_hbm, k_hbm, v_hbm,
          out, out_k, out_v,
          tables, lens, mig_req, emb, gain_attn, gain_out, res, turn,
          k_all, v_all, send_buf, recv_buf, fresh_send, fresh_recv,
          h32, h_in, ss_all, ss_out, fk, fv, q_buf, o_buf,
          small_sem, load_sem, mig_send, mig_recv, fresh_ssem, fresh_rsem,
          h_ssem, h_rsem, ss_ssem, ss_rsem, peer_sem):
    sections = lax.axis_size("section")
    cores = lax.axis_size("tp")
    section = lax.axis_index("section")
    core = lax.axis_index("tp")
    inst = lax.axis_index("inst")
    steps, requests, width = emb.shape
    pool, blk, kv_local = k_all.shape
    maxblk = tables.shape[2]
    heads_kv = kv_local // HD
    group = QH // KVH
    rows = group * steps
    scale = HD ** (-0.5)
    total_width = width * cores
    source = jnp.bitwise_xor(inst, offset)

    part = pool // LOADS
    loads = []
    for which, (src, dst) in enumerate(((k_hbm, k_all), (v_hbm, v_all))):
        for i in range(LOADS):
            span = pl.ds(i * part, part)
            loads.append(pltpu.make_async_copy(src.at[0, 0, span], dst.at[span], load_sem.at[which, i]))
    small = []
    for i, (src, dst) in enumerate((
            (tables_hbm, tables), (mig_hbm, mig_req), (lens_hbm, lens),
            (emb_hbm, emb), (gain_attn_hbm, gain_attn), (gain_out_hbm, gain_out))):
        small.append(pltpu.make_async_copy(src, dst, small_sem.at[i]))
    for copy in small[:2] + loads[:LOADS] + small[2:]:
        copy.start()

    barrier = pltpu.get_barrier_semaphore()
    pl.semaphore_signal(barrier, inc=1, device_id={"inst": source}, device_id_type=MESH)
    for step in range(1, cores):
        pl.semaphore_signal(barrier, inc=1, device_id={"tp": lax.rem(core + step, cores)}, device_id_type=MESH)

    @pl.when(section > 0)
    def _():
        for other in range(cores):
            pl.semaphore_signal(barrier, inc=1, device_id={"section": section - 1, "tp": other}, device_id_type=MESH)

    @pl.when(section < sections - 1)
    def _():
        for other in range(cores):
            pl.semaphore_signal(barrier, inc=1, device_id={"section": section + 1, "tp": other}, device_id_type=MESH)

    neighbours = jnp.minimum(section, 1) + jnp.minimum(sections - 1 - section, 1)
    pl.semaphore_wait(barrier, cores * (1 + neighbours))

    def peer_copy(r, step):
        return pltpu.make_async_remote_copy(
            src_ref=ss_all.at[core, r], dst_ref=ss_all.at[core, r],
            send_sem=peer_sem.at[r, step], recv_sem=ss_rsem.at[r, core],
            device_id={"tp": lax.rem(core + step, cores)}, device_id_type=MESH)

    def next_copy(r):
        return pltpu.make_async_remote_copy(
            src_ref=res.at[r], dst_ref=h_in.at[r],
            send_sem=h_ssem.at[r], recv_sem=h_rsem.at[r],
            device_id={"section": section + 1}, device_id_type=MESH)

    def next_sum(r, other):
        return pltpu.make_async_remote_copy(
            src_ref=ss_out.at[r], dst_ref=ss_all.at[core, r],
            send_sem=ss_ssem.at[r, other], recv_sem=ss_rsem.at[r, core],
            device_id={"section": section + 1, "tp": other}, device_id_type=MESH)

    def sum_arrival(r, other):
        return pltpu.make_async_remote_copy(
            src_ref=ss_out.at[r], dst_ref=ss_all.at[other, r],
            send_sem=ss_ssem.at[r, other], recv_sem=ss_rsem.at[r, other],
            device_id={"tp": lax.rem(core + 1, cores)}, device_id_type=MESH)

    def mig_copy(which, b):
        return pltpu.make_async_remote_copy(
            src_ref=send_buf.at[which, b], dst_ref=recv_buf.at[which, b],
            send_sem=mig_send.at[which, b], recv_sem=mig_recv.at[which, b],
            device_id={"inst": source}, device_id_type=MESH)

    fresh_copy = pltpu.make_async_remote_copy(
        src_ref=fresh_send, dst_ref=fresh_recv, send_sem=fresh_ssem, recv_sem=fresh_rsem,
        device_id={"inst": source}, device_id_type=MESH)

    for copy in small[:2]:
        copy.wait()
    handed = mig_req[inst]
    held = maxblk // 2
    for which, stored in enumerate((k_all, v_all)):
        for i in range(LOADS):
            loads[which * LOADS + i].wait()
        if which == 0:
            for copy in loads[LOADS:]:
                copy.start()

        def send_block(b, carry, which=which, stored=stored):
            send_buf[which, b] = stored[tables[0, handed, b]]
            mig_copy(which, b).start()
            return carry
        lax.fori_loop(0, maxblk if which == 0 else maxblk - held, send_block, 0)

    for copy in small[2:]:
        copy.wait()

    @pl.when(section == 0)
    def _():
        for t in range(steps):
            e = emb[t].astype(jnp.float32)
            for r in range(requests):
                h32[r, t:t + 1, :] = e[r:r + 1, :]
        for r in range(requests):
            h = h32[r]
            ss_all[core, r] = jnp.broadcast_to(jnp.sum(h * h, axis=-1, keepdims=True), (steps, HD))
        for r in range(requests):
            for step in range(1, cores):
                peer_copy(r, step).start()

    fk[...] = jnp.zeros_like(fk)
    fv[...] = jnp.zeros_like(fv)

    def one_request(r, carry):
        @pl.when(section == 0)
        def _():
            for step in range(1, cores):
                sum_arrival(r, lax.rem(core + step, cores)).wait_recv()

        @pl.when(section > 0)
        def _():
            next_copy(r).wait_recv()
            for other in range(cores):
                sum_arrival(r, other).wait_recv()
            h32[r] = h_in[r].astype(jnp.float32)

        squares = ss_all[0, r]
        for other in range(1, cores):
            squares = squares + ss_all[other, r]
        ratio = lax.rsqrt(squares / total_width + 1e-05)
        length = lens[inst, r]
        for g in range(heads_kv):
            key_sum = jnp.zeros((steps, HD), jnp.float32)
            value_sum = jnp.zeros((steps, HD), jnp.float32)
            for j in range(group):
                lanes = slice((g * group + j) * HD, (g * group + j + 1) * HD)
                hj = h32[r, :, lanes]
                xj = hj * ratio * gain_attn[0:1, lanes]
                q_buf[g, j * steps:(j + 1) * steps, :] = xj
                key_sum = key_sum + xj
                value_sum = value_sum + hj
            fk[r, 0:steps, g * HD:(g + 1) * HD] = key_sum * (1.0 / group)
            fv[r, 0:steps, g * HD:(g + 1) * HD] = value_sum * (1.0 / group)
        col = lax.broadcasted_iota(jnp.int32, (rows, blk), 1)
        new_col = lax.broadcasted_iota(jnp.int32, (rows, PAD), 1)
        new_step = lax.rem(lax.broadcasted_iota(jnp.int32, (rows, PAD), 0), steps)
        for g in range(heads_kv):
            lanes = slice(g * HD, (g + 1) * HD)
            q = q_buf[g].astype(jnp.bfloat16)
            nt = (((1,), (1,)), ((), ()))
            scores = []
            for b in range(maxblk):
                kb = k_all[tables[0, r, b], :, lanes]
                s = lax.dot_general(q, kb, nt, preferred_element_type=jnp.float32) * scale
                scores.append(jnp.where(col + b * blk < length, s, -jnp.inf))
            new = lax.dot_general(q, fk[r, :, lanes].astype(jnp.bfloat16), nt, preferred_element_type=jnp.float32) * scale
            new = jnp.where(new_col <= new_step, new, -jnp.inf)
            top = functools.reduce(jnp.maximum, scores)
            top = jnp.maximum(jnp.max(top, axis=-1, keepdims=True), jnp.max(new, axis=-1, keepdims=True))
            expo = [jnp.exp(s - top) for s in scores]
            expo_new = jnp.exp(new - top)
            total = jnp.sum(functools.reduce(jnp.add, expo), axis=-1, keepdims=True)
            total = total + jnp.sum(expo_new, axis=-1, keepdims=True)
            inverse = 1.0 / total
            o = jnp.dot((expo_new * inverse).astype(jnp.bfloat16), fv[r, :, lanes].astype(jnp.bfloat16),
                        preferred_element_type=jnp.float32)
            for b in range(maxblk):
                vb = v_all[tables[0, r, b], :, lanes]
                o = o + jnp.dot((expo[b] * inverse).astype(jnp.bfloat16), vb, preferred_element_type=jnp.float32)
            o_buf[g] = o * lax.rsqrt(jnp.mean(o * o, axis=-1, keepdims=True) + 1e-05)
        sums = jnp.zeros((steps, HD), jnp.float32)
        for g in range(heads_kv):
            for j in range(group):
                lanes = slice((g * group + j) * HD, (g * group + j + 1) * HD)
                y = h32[r, :, lanes] + o_buf[g, j * steps:(j + 1) * steps, :] * gain_out[0:1, lanes]
                y = y.astype(jnp.bfloat16)
                res[r, :, lanes] = y
                y = y.astype(jnp.float32)
                sums = sums + y * y
        ss_out[r] = jnp.broadcast_to(jnp.sum(sums, axis=-1, keepdims=True), (steps, HD))

        @pl.when(section < sections - 1)
        def _():
            next_copy(r).start()
            for other in range(cores):
                next_sum(r, other).start()
        return carry

    lax.fori_loop(0, requests, one_request, 0)

    fresh_send[0] = fk[handed].astype(jnp.bfloat16)
    fresh_send[1] = fv[handed].astype(jnp.bfloat16)
    fresh_copy.start()

    def send_held(b, carry):
        send_buf[1, b] = v_all[tables[0, handed, b]]
        mig_copy(1, b).start()
        return carry
    lax.fori_loop(maxblk - held, maxblk, send_held, 0)
    for r in range(requests):
        y = res[r].astype(jnp.float32)
        for t in range(steps):
            turn[t, r:r + 1, :] = y[t:t + 1, :]
    out[0] = turn[...].astype(jnp.bfloat16)
    fresh_copy.wait_recv()
    source_len = lens[source, mig_req[source]]

    for which in range(2):
        def settle(b, carry, which=which):
            mig_copy(which, b).wait_recv()
            pos = lax.broadcasted_iota(jnp.int32, (blk, PAD), 0) + b * blk - source_len
            hit = jnp.where(pos == lax.broadcasted_iota(jnp.int32, (blk, PAD), 1), 1.0, 0.0).astype(jnp.bfloat16)
            placed = jnp.dot(hit, fresh_recv[which], preferred_element_type=jnp.float32)
            row = lax.broadcasted_iota(jnp.int32, (blk, kv_local), 0) + b * blk
            block = jnp.where(row < source_len, recv_buf[which, b].astype(jnp.float32), placed)
            target = (out_k, out_v)[which]
            target[0, 0, pl.ds(pl.multiple_of(b * blk, blk), blk), :] = block.astype(jnp.bfloat16)
            return carry
        lax.fori_loop(0, maxblk, settle, 0)

    for which in range(2):
        def finish(b, carry, which=which):
            mig_copy(which, b).wait_send()
            return carry
        lax.fori_loop(0, maxblk, finish, 0)
    fresh_copy.wait_send()

    @pl.when(section == 0)
    def _():
        for r in range(requests):
            for step in range(1, cores):
                peer_copy(r, step).wait_send()

    @pl.when(section < sections - 1)
    def _():
        for r in range(requests):
            next_copy(r).wait_send()
            for other in range(cores):
                next_sum(r, other).wait_send()


def store(res, k, v, res_out, k_out, v_out, sems, res_sem):
    part = k.shape[2] // STORES
    copies = [pltpu.make_async_copy(res, res_out, res_sem)]
    for which, (src, dst) in enumerate(((k, k_out), (v, v_out))):
        for i in range(STORES):
            span = pl.ds(i * part, part)
            copies.append(pltpu.make_async_copy(src.at[0, 0, span], dst.at[0, 0, span], sems.at[which, i]))
    for copy in copies:
        copy.start()
    for copy in copies:
        copy.wait()


def local(emb, attn_gain, out_gain, k_cache, v_cache, tables, lens, partner, mig_req):
    steps, requests, width = emb.shape
    _, _, pool, blk, kv_local = k_cache.shape
    maxblk = tables.shape[2]
    cores = lax.axis_size("tp")
    context = maxblk * blk
    rows = QH // KVH * steps
    heads_kv = kv_local // HD
    bf16, f32 = jnp.bfloat16, jnp.float32
    vmem = pl.BlockSpec(memory_space=pltpu.VMEM)
    anywhere = pl.BlockSpec(memory_space=pl.ANY)
    dma = pltpu.SemaphoreType.DMA

    def call(offset):
        return pl.pallas_call(
            functools.partial(fused, offset),
            out_shape=(
                jax.ShapeDtypeStruct((1, steps, requests, width), bf16),
                jax.ShapeDtypeStruct((1, 1, context, kv_local), bf16),
                jax.ShapeDtypeStruct((1, 1, context, kv_local), bf16),
            ),
            in_specs=[anywhere] * 8,
            out_specs=(vmem, vmem, vmem),
            scratch_shapes=[
                pltpu.SMEM(tables.shape, jnp.int32),
                pltpu.SMEM(lens.shape, jnp.int32),
                pltpu.SMEM(mig_req.shape, jnp.int32),
                pltpu.VMEM(emb.shape, bf16),
                pltpu.VMEM(attn_gain.shape, f32),
                pltpu.VMEM(out_gain.shape, f32),
                pltpu.VMEM((requests, steps, width), bf16),
                pltpu.VMEM((steps, requests, width), f32),
                pltpu.VMEM((pool, blk, kv_local), bf16),
                pltpu.VMEM((pool, blk, kv_local), bf16),
                pltpu.VMEM((2, maxblk, blk, kv_local), bf16),
                pltpu.VMEM((2, maxblk, blk, kv_local), bf16),
                pltpu.VMEM((2, PAD, kv_local), bf16),
                pltpu.VMEM((2, PAD, kv_local), bf16),
                pltpu.VMEM((requests, steps, width), f32),
                pltpu.VMEM((requests, steps, width), bf16),
                pltpu.VMEM((cores, requests, steps, HD), f32),
                pltpu.VMEM((requests, steps, HD), f32),
                pltpu.VMEM((requests, PAD, kv_local), f32),
                pltpu.VMEM((requests, PAD, kv_local), f32),
                pltpu.VMEM((heads_kv, rows, HD), f32),
                pltpu.VMEM((heads_kv, rows, HD), f32),
                dma((6,)),
                dma((2, LOADS)),
                dma((2, maxblk)),
                dma((2, maxblk)),
                dma,
                dma,
                dma((requests,)),
                dma((requests,)),
                dma((requests, cores)),
                dma((requests, cores)),
                dma((requests, cores)),
            ],
            compiler_params=pltpu.CompilerParams(collective_id=offset, has_side_effects=True),
        )

    offsets = lax.axis_size("inst") - 1
    branches = [call(offset) for offset in range(1, offsets + 1)]
    chosen = jnp.clip(partner[0] - 1, 0, offsets - 1)
    results = lax.switch(
        chosen, branches, tables, lens, mig_req, emb, attn_gain, out_gain, k_cache, v_cache)
    return pl.pallas_call(
        store,
        out_shape=tuple(jax.ShapeDtypeStruct(a.shape, a.dtype) for a in results),
        in_specs=[anywhere] * 3,
        out_specs=(anywhere,) * 3,
        scratch_shapes=[dma((2, STORES)), dma],
    )(*results)


def solution(mesh):
    return jax.shard_map(
        local,
        mesh=mesh,
        in_specs=(
            P(None, ("groups", "inst"), "tp"),
            P("section", "tp"),
            P("section", "tp"),
            P(("groups", "inst"), "section", None, None, "tp"),
            P(("groups", "inst"), "section", None, None, "tp"),
            P(("groups", "inst"), None, None),
            P("groups", None),
            P(),
            P("groups"),
        ),
        out_specs=(
            P("section", None, ("groups", "inst"), "tp"),
            P(("groups", "inst"), "section", None, "tp"),
            P(("groups", "inst"), "section", None, "tp"),
        ),
        check_vma=False,
    )
```
